128 devices in a mesh: dp: 8 (over y, core), ctx: 16 (over z, x).
Axes of the slice: x: 4, y: 4, z: 4, core: 2. Of those that a mesh axis runs over, the one named last changes fastest.
Arguments:
- query_act: bfloat16 [8, 2048, 8192], P('dp', 'ctx'), may hold values from -6 to 6
- key_act: bfloat16 [8, 2048, 8192], P('dp', 'ctx'), may hold values from -6 to 6
- value_act: bfloat16 [8, 2048, 8192], P('dp', 'ctx'), may hold values from -6 to 6
- grad_out: bfloat16 [8, 2048, 8192], P('dp', 'ctx'), may hold values from -6 to 6
- filter_taps: float32 [2048, 8192], P('ctx'), may hold values from -0.125 to 0.125
Outputs:
- grad_query: bfloat16 [8, 2048, 8192], P('dp', 'ctx')
- grad_key: bfloat16 [8, 2048, 8192], P('dp', 'ctx')
- grad_value: bfloat16 [8, 2048, 8192], P('dp', 'ctx')
- grad_filter: float32 [2048, 8192], P('dp', 'ctx')
The draws below stay inside these ranges and needn't reach their ends.
All inputs are finite; a program needn't handle non-finite values.
Results may differ from the reference program's by a relative error of at most 0.017.
Values may be sent and summed in bfloat16 or wider, within the bound.
No kernel may reach another device: no remote copies, remote signals or barrier semaphores. Data moves between devices by JAX's collectives and lax.ppermute only.
A program may use at most 256 MiB of HBM per device.

```python
import jax
import jax.numpy as jnp
from jax import lax

D = 8192
SEQ = 2048
FFT_N = 4096
SEQS = 8


def block_scale(key, shape, pieces, low, high):
    level, own = 1.0, jax.random.fold_in(key, 6)
    for axis_at, shards_of in pieces:
        steps = jnp.exp(jax.random.uniform(jax.random.fold_in(own, axis_at), (shards_of,), jnp.float32, low / len(pieces), high / len(pieces)))
        level = level * jnp.repeat(steps, shape[axis_at] // shards_of).reshape([-1 if axis == axis_at else 1 for axis in range(len(shape))])
    return level


def gaussian(key, extent, deviation, most, cuts=(), kind=jnp.bfloat16):
    entries = deviation * jax.random.normal(key, extent, jnp.float32)
    if cuts:
        entries = entries * block_scale(key, extent, cuts, -0.22, 0.18)
    return jnp.clip(entries, -most, most).astype(kind)


def setup_inputs(seed: int = 0) -> dict:
    key_list = jax.random.split(jax.random.key(seed), 6)
    query_act = gaussian(key_list[0], (SEQS, SEQ, D), 1.0, 6.0, ((0, 8), (1, 16)))
    key_act = gaussian(key_list[1], (SEQS, SEQ, D), 1.0, 6.0, ((0, 8), (1, 16)))
    value_act = gaussian(key_list[2], (SEQS, SEQ, D), 1.0, 6.0, ((0, 8), (1, 16)))
    grad_out = gaussian(key_list[3], (SEQS, SEQ, D), 1.0, 6.0, ((0, 8), (1, 16)))
    filter_taps = gaussian(key_list[4], (SEQ, D), SEQ ** -0.5, 0.125, ((0, 16),), jnp.float32)
    return {"query_act": query_act, "key_act": key_act, "value_act": value_act, "grad_out": grad_out, "filter_taps": filter_taps}


def reference(query_act, key_act, value_act, grad_out, filter_taps):
    product = (key_act.astype(jnp.float32) * value_act.astype(jnp.float32)).astype(jnp.bfloat16)
    gated_grad = (grad_out.astype(jnp.float32) * query_act.astype(jnp.float32)).astype(jnp.bfloat16)
    taps_spec = jnp.fft.rfft(filter_taps.astype(jnp.float32), n=FFT_N, axis=0)

    def per_sequence(total, pair):
        prod_one, grad_one = pair
        prod_spec = jnp.fft.rfft(prod_one.astype(jnp.float32), n=FFT_N, axis=0)
        grad_spec = jnp.fft.rfft(grad_one.astype(jnp.float32), n=FFT_N, axis=0)
        conv_out = jnp.fft.irfft(taps_spec * prod_spec, n=FFT_N, axis=0)[:SEQ].astype(jnp.bfloat16)
        back_grad = jnp.fft.irfft(jnp.conj(taps_spec) * grad_spec, n=FFT_N, axis=0)[:SEQ].astype(jnp.bfloat16)
        taps_grad = jnp.fft.irfft(jnp.conj(prod_spec) * grad_spec, n=FFT_N, axis=0)[:SEQ]
        return total + taps_grad.astype(jnp.float32), (conv_out, back_grad)

    grad_filter, outputs = lax.scan(per_sequence, jnp.zeros((SEQ, D), jnp.float32), (product, gated_grad))
    conv_all, back_all = outputs
    grad_query = (grad_out.astype(jnp.float32) * conv_all.astype(jnp.float32)).astype(jnp.bfloat16)
    grad_key = (back_all.astype(jnp.float32) * value_act.astype(jnp.float32)).astype(jnp.bfloat16)
    grad_value = (back_all.astype(jnp.float32) * key_act.astype(jnp.float32)).astype(jnp.bfloat16)
    return (grad_query, grad_key, grad_value, grad_filter)
```

```python
import functools

import jax
import jax.numpy as jnp
from jax import lax
from jax.experimental import pallas as pl
from jax.experimental.pallas import tpu as pltpu
from jax.sharding import PartitionSpec as P

LANES = 128
NT = (((1,), (1,)), ((), ()))


def params(mib):
    return pltpu.CompilerParams(vmem_limit_bytes=mib * 1024 * 1024)


def grid_of(shape):
    return lax.broadcasted_iota(jnp.int32, shape, 0), lax.broadcasted_iota(jnp.int32, shape, 1)


def ones_where(condition):
    return jnp.where(condition, 1.0, 0.0).astype(jnp.bfloat16)


def identity():
    rows, cols = grid_of((LANES, LANES))
    return ones_where(rows == cols)


def reversal():
    rows, cols = grid_of((LANES, LANES))
    return ones_where(rows + cols == LANES - 1)


def turn(matrix, array):
    return lax.dot_general(matrix, array, NT, preferred_element_type=jnp.float32)


def gate(left, right):
    return (left.astype(jnp.float32) * right.astype(jnp.float32)).astype(jnp.bfloat16)


def send_body(local, share, key_ref, value_ref, grad_ref, query_ref, taps_ref, out_ref):
    per = LANES // local
    same = identity()
    rows, cols = grid_of((per * share, LANES))
    first = lax.axis_index("dp") * share
    pick = ones_where(cols == rows // share * local + first + rows % share)
    for g in range(key_ref.shape[1] // LANES):
        at = slice(g * LANES, (g + 1) * LANES)
        product = turn(same, gate(key_ref[:, at], value_ref[:, at])).astype(jnp.bfloat16)
        gated = turn(same, gate(grad_ref[:, at], query_ref[:, at])).astype(jnp.bfloat16)
        taps = turn(pick, taps_ref[:, at].astype(jnp.bfloat16)).astype(jnp.bfloat16)
        for d in range(per):
            dest = g * per + d
            out_ref[dest, :local, :] = product[d * local : (d + 1) * local]
            out_ref[dest, local : 2 * local, :] = gated[d * local : (d + 1) * local]
            out_ref[dest, 2 * local :, :] = taps[d * share : (d + 1) * share]


def send(key, value, grad, query, taps, local, share):
    length, channels = key.shape
    width = 2048
    message = 2 * local + share
    spec = pl.BlockSpec((length, width), lambda g: (0, g))
    return pl.pallas_call(
        functools.partial(send_body, local, share),
        grid=(channels // width,),
        in_specs=[spec] * 5,
        out_specs=pl.BlockSpec((width // local, message, LANES), lambda g: (g, 0, 0)),
        out_shape=jax.ShapeDtypeStruct((channels // local, message, LANES), jnp.bfloat16),
        compiler_params=params(60),
        cost_estimate=pl.CostEstimate(flops=0, bytes_accessed=20_000_000, transcendentals=0),
        name="send",
    )(key, value, grad, query, taps)


def both_body(
    local, share, seqs, group, prod_ref, grad_ref, taps_ref, out_ref, prod_wide, grad_wide, taps_wide, taps
):
    rows = prod_ref.shape[0]
    blocks = rows // seqs
    flip = reversal()
    g = pl.program_id(0)

    @pl.when(g == 0)
    def _():
        taps_wide[...] = taps_ref[...].astype(jnp.float32).reshape(rows * share, LANES)
        for c in range(local):
            taps[c * blocks : (c + 1) * blocks, :] = taps_wide[pl.ds(c, blocks, stride=seqs * share), :]

    prod_wide[...] = prod_ref[...].astype(jnp.float32).reshape(rows * group, LANES)
    grad_wide[...] = jnp.dot(
        grad_ref[...].reshape(rows * group, LANES), flip, preferred_element_type=jnp.float32
    )
    row, lane = grid_of((LANES, LANES))
    same_block = lane >= row

    def step(c, carry):
        here = pl.ds(c, rows, stride=group)
        prod = prod_wide[here, :].astype(jnp.bfloat16)
        grad = grad_wide[here, :].astype(jnp.bfloat16)
        before = jnp.zeros((LANES, LANES), jnp.float32)
        conv = [None] * blocks
        back = [None] * blocks

        def add(sums, i, piece):
            sums[i] = piece if sums[i] is None else sums[i] + piece

        for k in range(0, blocks, 2):
            pair = []
            for near in (k, k + 1):
                line = taps[pl.ds((g * group + c) * blocks + near, 1), :]
                turned = pltpu.roll(
                    jnp.broadcast_to(line, (LANES, LANES)), 0, 1, stride=1, stride_axis=0
                )
                pair.append(jnp.where(same_block, turned, before).astype(jnp.bfloat16))
                before = turned
            used = rows - k * seqs
            lines = jnp.concatenate([prod[:used], grad[k * seqs :]], axis=0)
            part = jnp.dot(
                lines, jnp.concatenate(pair, axis=1), preferred_element_type=jnp.float32
            )
            for j in range(blocks - k):
                for side in (0, 1):
                    cols = slice(side * LANES, (side + 1) * LANES)
                    if j + k + side < blocks:
                        add(conv, j + k + side, part[j * seqs : (j + 1) * seqs, cols])
                    if j >= side:
                        add(back, j - side, part[used + j * seqs : used + (j + 1) * seqs, cols])
        prod_wide[here, :] = jnp.concatenate(conv, axis=0)
        grad_wide[here, :] = jnp.concatenate(back, axis=0)
        return carry

    lax.fori_loop(0, group, step, 0, unroll=True)
    out_ref[:, 0] = prod_wide[...].astype(jnp.bfloat16).reshape(rows, group, LANES)
    rounded = grad_wide[...].astype(jnp.bfloat16)
    out_ref[:, 1] = (
        jnp.dot(rounded, flip, preferred_element_type=jnp.float32)
        .astype(jnp.bfloat16)
        .reshape(rows, group, LANES)
    )


def both(received, local, share, seqs):
    rows = received.shape[0]
    blocks = rows // seqs
    group = 8
    steps = local // group
    return pl.pallas_call(
        functools.partial(both_body, local, share, seqs, group),
        grid=(steps,),
        in_specs=[
            pl.BlockSpec((rows, group, LANES), lambda g: (0, g, 0)),
            pl.BlockSpec((rows, group, LANES), lambda g: (0, steps + g, 0)),
            pl.BlockSpec((rows, share, LANES), lambda g: (0, 2 * local // share, 0)),
        ],
        out_specs=pl.BlockSpec((rows, 2, group, LANES), lambda g: (0, 0, g, 0)),
        out_shape=jax.ShapeDtypeStruct((rows, 2, local, LANES), jnp.bfloat16),
        scratch_shapes=[
            pltpu.VMEM((rows * group, LANES), jnp.float32),
            pltpu.VMEM((rows * group, LANES), jnp.float32),
            pltpu.VMEM((rows * share, LANES), jnp.float32),
            pltpu.VMEM((local * blocks, LANES), jnp.float32),
        ],
        compiler_params=params(40),
        cost_estimate=pl.CostEstimate(
            flops=20_000_000_000, bytes_accessed=10_000_000, transcendentals=0
        ),
        name="both",
    )(received, received, received)


def filter_body(local, seqs, group, prod_ref, grad_ref, out_ref, prod_wide, grad_wide, padded):
    rows = prod_ref.shape[0]
    blocks = rows // seqs
    flip = reversal()
    row, lane = grid_of((LANES, LANES))
    same_block = lane <= row
    prod_wide[...] = prod_ref[...].astype(jnp.float32).reshape(rows * group, LANES)
    grad_wide[...] = grad_ref[...].astype(jnp.float32).reshape(rows * group, LANES)
    padded[:, rows:, :] = jnp.zeros((2, rows, LANES), jnp.float32)

    def step(c, carry):
        here = pl.ds(c, rows, stride=group)
        lines = turn(flip, prod_wide[here, :].astype(jnp.bfloat16)).astype(jnp.bfloat16)
        slot = padded.at[c % 2]
        slot[:rows, :] = grad_wide[here, :]
        after = jnp.zeros((LANES, LANES), jnp.float32)
        for k in reversed(range(0, blocks, 2)):
            pair = jnp.concatenate(
                [
                    slot[near * seqs : near * seqs + rows, :].astype(jnp.bfloat16)
                    for near in (k, k + 1)
                ],
                axis=1,
            )
            part = jnp.dot(lines, pair, preferred_element_type=jnp.float32)
            for side in (1, 0):
                turned = pltpu.roll(
                    part[:, side * LANES : (side + 1) * LANES], 1, 1, stride=1, stride_axis=0
                )
                chosen = jnp.where(same_block, turned, after)
                out_ref[k + side, pl.ds(c, 1), :] = jnp.sum(chosen, axis=0, keepdims=True)
                after = turned
        return carry

    lax.fori_loop(0, group, step, 0, unroll=4)


def filter_grad(received, local, seqs):
    rows = received.shape[0]
    blocks = rows // seqs
    group = 8
    steps = local // group
    return pl.pallas_call(
        functools.partial(filter_body, local, seqs, group),
        grid=(steps,),
        in_specs=[
            pl.BlockSpec((rows, group, LANES), lambda g: (0, g, 0)),
            pl.BlockSpec((rows, group, LANES), lambda g: (0, steps + g, 0)),
        ],
        out_specs=pl.BlockSpec((blocks, group, LANES), lambda g: (0, g, 0)),
        out_shape=jax.ShapeDtypeStruct((blocks, local, LANES), jnp.float32),
        scratch_shapes=[
            pltpu.VMEM((rows * group, LANES), jnp.float32),
            pltpu.VMEM((rows * group, LANES), jnp.float32),
            pltpu.VMEM((2, 2 * rows, LANES), jnp.float32),
        ],
        compiler_params=params(40),
        cost_estimate=pl.CostEstimate(
            flops=25_000_000_000, bytes_accessed=10_000_000, transcendentals=0
        ),
        name="filter_grad",
    )(received, received)


def finish_body(local, in_ref, grad_ref, value_ref, key_ref, query_out, key_out, value_out):
    same = identity()
    per = LANES // local
    for g in range(grad_ref.shape[1] // LANES):
        at = slice(g * LANES, (g + 1) * LANES)
        block = in_ref[g * per : (g + 1) * per]
        conv = turn(same, block[:, 0].reshape(LANES, LANES))
        back = turn(same, block[:, 1].reshape(LANES, LANES))
        query_out[:, at] = (conv * grad_ref[:, at].astype(jnp.float32)).astype(jnp.bfloat16)
        key_out[:, at] = (back * value_ref[:, at].astype(jnp.float32)).astype(jnp.bfloat16)
        value_out[:, at] = (back * key_ref[:, at].astype(jnp.float32)).astype(jnp.bfloat16)


def finish(received, grad, value, key):
    parts, two, local, lanes = received.shape
    length, channels = key.shape
    width = 2048
    spec = pl.BlockSpec((length, width), lambda g: (0, g))
    shape = jax.ShapeDtypeStruct((length, channels), jnp.bfloat16)
    return pl.pallas_call(
        functools.partial(finish_body, local),
        grid=(channels // width,),
        in_specs=[pl.BlockSpec((width // local, two, local, lanes), lambda g: (g, 0, 0, 0))]
        + [spec] * 3,
        out_specs=(spec,) * 3,
        out_shape=(shape,) * 3,
        compiler_params=params(60),
        cost_estimate=pl.CostEstimate(flops=0, bytes_accessed=20_000_000, transcendentals=0),
        name="finish",
    )(received, grad, value, key)


def exchange(array):
    return lax.all_to_all(array, ("ctx", "dp"), split_axis=0, concat_axis=0, tiled=True)


def spread_lags(lags, seqs):
    me = lax.axis_index("dp")
    held = jnp.zeros_like(lags)
    for offset in range(seqs):
        piece = lax.dynamic_index_in_dim(lags, (me + offset) % seqs, 0, keepdims=True)
        if offset:
            piece = lax.ppermute(piece, "dp", [(s, (s + offset) % seqs) for s in range(seqs)])
        held = lax.dynamic_update_slice_in_dim(held, piece, (me - offset) % seqs, 0)
    return held


def on_device(seqs, blocks, query_act, key_act, value_act, grad_out, filter_taps):
    query, key, value, grad = query_act[0], key_act[0], value_act[0], grad_out[0]
    channels = key.shape[1]
    local = channels // (seqs * blocks)
    share = local // seqs
    received = exchange(send(key, value, grad, query, filter_taps, local, share))
    sums = both(received, local, share, seqs)
    returned = exchange(sums)
    received, sums = lax.optimization_barrier((received, sums))
    lags = filter_grad(received, local, seqs)
    lags = spread_lags(lags.reshape(seqs, blocks // seqs, local, LANES), seqs)
    grad_filter = lags.transpose(1, 3, 0, 2).reshape(blocks // seqs * LANES, seqs * local)
    grad_query, grad_key, grad_value = finish(returned, grad, value, key)
    return (grad_query[None], grad_key[None], grad_value[None], grad_filter)


def solution(mesh):
    seqs, blocks = mesh.shape["dp"], mesh.shape["ctx"]
    spec = P("dp", "ctx", None)
    return jax.shard_map(
        functools.partial(on_device, seqs, blocks),
        mesh=mesh,
        in_specs=(spec, spec, spec, spec, P("ctx", None)),
        out_specs=(spec, spec, spec, P("dp", "ctx")),
        check_vma=False,
    )
```

```python
import functools

import jax
import jax.numpy as jnp
from jax import lax
from jax.experimental import pallas as pl
from jax.experimental.pallas import tpu as pltpu
from jax.sharding import PartitionSpec as P

LANES = 128
NT = (((1,), (1,)), ((), ()))


def params(mib):
    return pltpu.CompilerParams(vmem_limit_bytes=mib * 1024 * 1024)


def grid_of(shape):
    return lax.broadcasted_iota(jnp.int32, shape, 0), lax.broadcasted_iota(jnp.int32, shape, 1)


def ones_where(condition):
    return jnp.where(condition, 1.0, 0.0).astype(jnp.bfloat16)


def identity():
    rows, cols = grid_of((LANES, LANES))
    return ones_where(rows == cols)


def reversal():
    rows, cols = grid_of((LANES, LANES))
    return ones_where(rows + cols == LANES - 1)


def turn(matrix, array):
    return lax.dot_general(matrix, array, NT, preferred_element_type=jnp.float32)


def gate(left, right):
    return (left.astype(jnp.float32) * right.astype(jnp.float32)).astype(jnp.bfloat16)


def send_body(local, share, me_ref, key_ref, value_ref, grad_ref, query_ref, low_ref, high_ref, out_ref):
    seqs = out_ref.shape[0]
    per = LANES // local
    same = identity()
    row, lane = grid_of((share, LANES))
    for g in range(key_ref.shape[1] // LANES):
        at = slice(g * LANES, (g + 1) * LANES)
        product = turn(same, gate(key_ref[:, at], value_ref[:, at])).astype(jnp.bfloat16)
        gated = turn(same, gate(grad_ref[:, at], query_ref[:, at])).astype(jnp.bfloat16)
        low, high = low_ref[:, at], high_ref[:, at]
        taps = (
            jnp.where(lane < local, low, pltpu.roll(high, local, 1)),
            jnp.where(lane < local, pltpu.roll(low, local, 1), high),
        )
        for d in range(per):
            x, s = divmod(g * per + d, seqs)
            out_ref[s, x, :local, :] = product[d * local : (d + 1) * local]
            out_ref[s, x, local : 2 * local, :] = gated[d * local : (d + 1) * local]
            out_ref[s, x, 2 * local :, :] = taps[d].astype(jnp.bfloat16)


def send(key, value, grad, query, taps, local, share, seqs):
    length, channels = key.shape
    width = 2048
    message = 2 * local + share
    wide = width // local // seqs
    spec = pl.BlockSpec((length, width), lambda g, me: (0, g))
    return pl.pallas_call(
        functools.partial(send_body, local, share),
        grid_spec=pltpu.PrefetchScalarGridSpec(
            num_scalar_prefetch=1,
            grid=(channels // width,),
            in_specs=[spec] * 4
            + [
                pl.BlockSpec((share, width), lambda g, me: (me[0], g)),
                pl.BlockSpec((share, width), lambda g, me: (seqs + me[0], g)),
            ],
            out_specs=pl.BlockSpec((seqs, wide, message, LANES), lambda g, me: (0, g, 0, 0)),
        ),
        out_shape=jax.ShapeDtypeStruct(
            (seqs, channels // local // seqs, message, LANES), jnp.bfloat16
        ),
        compiler_params=params(60),
        cost_estimate=pl.CostEstimate(flops=0, bytes_accessed=14_000_000, transcendentals=0),
        name="send",
    )(lax.axis_index("dp").astype(jnp.int32).reshape(1), key, value, grad, query, taps, taps)


def rows_of(wide, block, c, seqs, blocks, group):
    return pl.ds(block * group + c, seqs, stride=blocks * group)


def both_body(seqs, blocks, prod_ref, grad_ref, taps_ref, out_ref, prod_wide, grad_wide, taps):
    group = prod_ref.shape[2]
    local = LANES // 2
    share = taps_ref.shape[2]
    flip = reversal()
    g = pl.program_id(0)

    @pl.when(g == 0)
    def _():
        row, lane = grid_of((local, LANES))
        for j in range(0, blocks, 2):
            lags = jnp.concatenate(
                [taps_ref[b, j + side] for side in (0, 1) for b in range(seqs)], axis=0
            )
            lags = lags.astype(jnp.float32).T
            low, high = lags[:local], lags[local:]
            taps[pl.ds(j, local, stride=blocks), :] = jnp.where(
                lane < local, low, pltpu.roll(high, local, 1)
            )
            taps[pl.ds(j + 1, local, stride=blocks), :] = jnp.where(
                lane < local, pltpu.roll(low, local, 1), high
            )

    size = seqs * blocks * group
    prod_wide[...] = prod_ref[...].astype(jnp.float32).reshape(size, LANES)
    grad_wide[...] = jnp.dot(
        grad_ref[...].reshape(size, LANES), flip, preferred_element_type=jnp.float32
    )
    row, lane = grid_of((LANES, LANES))
    same_block = lane >= row
    pairs = blocks // 2

    def step(c, carry):
        def load(wide, block):
            return wide[rows_of(wide, block, c, seqs, blocks, group), :]

        tiles = []
        for i in range(pairs):
            o = pairs - 1 - i
            first = jnp.concatenate([load(prod_wide, 2 * i), load(prod_wide, 2 * i + 1)], axis=1)
            second = jnp.concatenate([load(grad_wide, 2 * o + 1), load(grad_wide, 2 * o)], axis=1)
            tiles.append(jnp.concatenate([first, second], axis=0).astype(jnp.bfloat16))
        lines = jnp.concatenate(tiles, axis=0)
        turned_before = jnp.zeros((LANES, LANES), jnp.float32)
        before = jnp.zeros((LANES, LANES), jnp.bfloat16)
        conv = [None] * pairs
        back = [None] * pairs

        def add(sums, i, piece):
            sums[i] = piece if sums[i] is None else sums[i] + piece

        for k in range(pairs):
            here = []
            for near in (2 * k, 2 * k + 1):
                line = taps[pl.ds((g * group + c) * blocks + near, 1), :]
                turned = pltpu.roll(
                    jnp.broadcast_to(line, (LANES, LANES)), 0, 1, stride=1, stride_axis=0
                )
                here.append(jnp.where(same_block, turned, turned_before).astype(jnp.bfloat16))
                turned_before = turned
            right = jnp.concatenate(
                [
                    jnp.concatenate(here, axis=1),
                    jnp.concatenate([before, here[0]], axis=1),
                ],
                axis=0,
            )
            before = here[1]
            part = jnp.dot(
                lines[: (pairs - k) * 2 * seqs], right, preferred_element_type=jnp.float32
            )
            for i in range(pairs - k):
                at = i * 2 * seqs
                add(conv, i + k, part[at : at + seqs])
                add(back, pairs - 1 - i - k, part[at + seqs : at + 2 * seqs])
        for i in range(pairs):
            for side in (0, 1):
                here = rows_of(prod_wide, 2 * i + side, c, seqs, blocks, group)
                prod_wide[here, :] = conv[i][:, side * LANES : (side + 1) * LANES]
                grad_wide[here, :] = back[i][:, (1 - side) * LANES : (2 - side) * LANES]
        return carry

    lax.fori_loop(0, group, step, 0, unroll=True)
    shape = (seqs, blocks, group, LANES)
    out_ref[:, :, 0] = prod_wide[...].astype(jnp.bfloat16).reshape(shape)
    rounded = grad_wide[...].astype(jnp.bfloat16)
    out_ref[:, :, 1] = (
        jnp.dot(rounded, flip, preferred_element_type=jnp.float32).astype(jnp.bfloat16).reshape(shape)
    )


def both(received, local, share):
    seqs, blocks = received.shape[:2]
    group = 8
    steps = local // group
    size = seqs * blocks * group
    return pl.pallas_call(
        functools.partial(both_body, seqs, blocks),
        grid=(steps,),
        in_specs=[
            pl.BlockSpec((seqs, blocks, group, LANES), lambda g: (0, 0, g, 0)),
            pl.BlockSpec((seqs, blocks, group, LANES), lambda g: (0, 0, steps + g, 0)),
            pl.BlockSpec((seqs, blocks, share, LANES), lambda g: (0, 0, 2 * local // share, 0)),
        ],
        out_specs=pl.BlockSpec((seqs, blocks, 2, group, LANES), lambda g: (0, 0, 0, g, 0)),
        out_shape=jax.ShapeDtypeStruct((seqs, blocks, 2, local, LANES), jnp.bfloat16),
        scratch_shapes=[
            pltpu.VMEM((size, LANES), jnp.float32),
            pltpu.VMEM((size, LANES), jnp.float32),
            pltpu.VMEM((local * blocks, LANES), jnp.float32),
        ],
        compiler_params=params(60),
        cost_estimate=pl.CostEstimate(
            flops=20_000_000_000, bytes_accessed=10_000_000, transcendentals=0
        ),
        name="both",
    )(received, received, received)


def filter_body(seqs, blocks, prod_ref, grad_ref, out_ref, prod_wide, grad_wide):
    group = prod_ref.shape[2]
    size = seqs * blocks * group
    flip = reversal()
    row, lane = grid_of((LANES, LANES))
    same_block = lane <= row
    prod_wide[...] = prod_ref[...].astype(jnp.float32).reshape(size, LANES)
    grad_wide[...] = grad_ref[...].astype(jnp.float32).reshape(size, LANES)
    nothing = jnp.zeros((seqs, LANES), jnp.float32)

    def step(c, carry):
        def load(wide, block):
            return wide[rows_of(wide, block, c, seqs, blocks, group), :]

        prod = jnp.concatenate([load(prod_wide, j) for j in range(blocks)], axis=0)
        lines = turn(flip, prod.astype(jnp.bfloat16)).astype(jnp.bfloat16)
        grad = [load(grad_wide, j) for j in range(blocks)] + [nothing] * 2
        twos = [
            jnp.concatenate([grad[j], grad[j + 1]], axis=0).astype(jnp.bfloat16)
            for j in range(blocks + 1)
        ]

        def shifted(k):
            return jnp.concatenate(
                [twos[min(j + k, blocks)] for j in range(0, blocks, 2)], axis=0
            )

        after = jnp.zeros((LANES, LANES), jnp.float32)
        for k in reversed(range(0, blocks, 2)):
            pair = jnp.concatenate([shifted(k), shifted(k + 1)], axis=1)
            part = jnp.dot(lines, pair, preferred_element_type=jnp.float32)
            for side in (1, 0):
                turned = pltpu.roll(
                    part[:, side * LANES : (side + 1) * LANES], 1, 1, stride=1, stride_axis=0
                )
                chosen = jnp.where(same_block, turned, after)
                out_ref[k + side, pl.ds(c, 1), :] = jnp.sum(chosen, axis=0, keepdims=True)
                after = turned
        return carry

    lax.fori_loop(0, group, step, 0, unroll=4)


def filter_grad(received, local):
    seqs, blocks = received.shape[:2]
    group = 8
    steps = local // group
    size = seqs * blocks * group
    return pl.pallas_call(
        functools.partial(filter_body, seqs, blocks),
        grid=(steps,),
        in_specs=[
            pl.BlockSpec((seqs, blocks, group, LANES), lambda g: (0, 0, g, 0)),
            pl.BlockSpec((seqs, blocks, group, LANES), lambda g: (0, 0, steps + g, 0)),
        ],
        out_specs=pl.BlockSpec((blocks, group, LANES), lambda g: (0, g, 0)),
        out_shape=jax.ShapeDtypeStruct((blocks, local, LANES), jnp.float32),
        scratch_shapes=[pltpu.VMEM((size, LANES), jnp.float32)] * 2,
        compiler_params=params(16),
        cost_estimate=pl.CostEstimate(
            flops=25_000_000_000, bytes_accessed=10_000_000, transcendentals=0
        ),
        name="filter_grad",
    )(received, received)


def finish_body(local, in_ref, grad_ref, value_ref, key_ref, query_out, key_out, value_out):
    same = identity()
    per = LANES // local
    seqs = in_ref.shape[0]
    for g in range(grad_ref.shape[1] // LANES):
        at = slice(g * LANES, (g + 1) * LANES)
        places = [divmod(g * per + d, seqs) for d in range(per)]
        conv = turn(same, jnp.concatenate([in_ref[s, x, 0] for x, s in places], axis=0))
        back = turn(same, jnp.concatenate([in_ref[s, x, 1] for x, s in places], axis=0))
        query_out[:, at] = (conv * grad_ref[:, at].astype(jnp.float32)).astype(jnp.bfloat16)
        key_out[:, at] = (back * value_ref[:, at].astype(jnp.float32)).astype(jnp.bfloat16)
        value_out[:, at] = (back * key_ref[:, at].astype(jnp.float32)).astype(jnp.bfloat16)


def finish(received, grad, value, key):
    seqs, blocks, two, local, lanes = received.shape
    length, channels = key.shape
    width = 2048
    spec = pl.BlockSpec((length, width), lambda g: (0, g))
    shape = jax.ShapeDtypeStruct((length, channels), jnp.bfloat16)
    return pl.pallas_call(
        functools.partial(finish_body, local),
        grid=(channels // width,),
        in_specs=[
            pl.BlockSpec(
                (seqs, width // local // seqs, two, local, lanes), lambda g: (0, g, 0, 0, 0)
            )
        ]
        + [spec] * 3,
        out_specs=(spec,) * 3,
        out_shape=(shape,) * 3,
        compiler_params=params(60),
        cost_estimate=pl.CostEstimate(flops=0, bytes_accessed=20_000_000, transcendentals=0),
        name="finish",
    )(received, grad, value, key)


def exchange(array):
    seqs, blocks, *rest = array.shape
    flat = array.reshape(seqs * blocks, *rest)
    moved = lax.all_to_all(flat, ("dp", "ctx"), split_axis=0, concat_axis=0, tiled=True)
    return moved.reshape(array.shape)


def spread_lags(lags, seqs):
    me = lax.axis_index("dp")
    held = jnp.zeros_like(lags)
    for offset in range(seqs):
        piece = lax.dynamic_index_in_dim(lags, (me + offset) % seqs, 0, keepdims=True)
        if offset:
            piece = lax.ppermute(piece, "dp", [(s, (s + offset) % seqs) for s in range(seqs)])
        held = lax.dynamic_update_slice_in_dim(held, piece, (me - offset) % seqs, 0)
    return held


def on_device(seqs, blocks, query_act, key_act, value_act, grad_out, filter_taps):
    query, key, value, grad = query_act[0], key_act[0], value_act[0], grad_out[0]
    channels = key.shape[1]
    local = channels // (seqs * blocks)
    share = local // seqs
    received = exchange(send(key, value, grad, query, filter_taps, local, share, seqs))
    sums = both(received, local, share)
    returned = exchange(sums)
    received, sums = lax.optimization_barrier((received, sums))
    lags = filter_grad(received, local)
    lags = spread_lags(lags.reshape(seqs, blocks // seqs, local, LANES), seqs)
    grad_filter = lags.transpose(1, 3, 0, 2).reshape(blocks // seqs * LANES, seqs * local)
    grad_query, grad_key, grad_value = finish(returned, grad, value, key)
    return (grad_query[None], grad_key[None], grad_value[None], grad_filter)


def solution(mesh):
    seqs, blocks = mesh.shape["dp"], mesh.shape["ctx"]
    spec = P("dp", "ctx", None)
    return jax.shard_map(
        functools.partial(on_device, seqs, blocks),
        mesh=mesh,
        in_specs=(spec, spec, spec, spec, P("ctx", None)),
        out_specs=(spec, spec, spec, P("dp", "ctx")),
        check_vma=False,
    )
```

```python
import functools

import jax
import jax.numpy as jnp
from jax import lax
from jax.experimental import pallas as pl
from jax.experimental.pallas import tpu as pltpu
from jax.sharding import PartitionSpec as P

LANES = 128
NT = (((1,), (1,)), ((), ()))


def params(mib):
    return pltpu.CompilerParams(vmem_limit_bytes=mib * 1024 * 1024)


def grid_of(shape):
    return lax.broadcasted_iota(jnp.int32, shape, 0), lax.broadcasted_iota(jnp.int32, shape, 1)


def ones_where(condition):
    return jnp.where(condition, 1.0, 0.0).astype(jnp.bfloat16)


def identity():
    rows, cols = grid_of((LANES, LANES))
    return ones_where(rows == cols)


def reversal():
    rows, cols = grid_of((LANES, LANES))
    return ones_where(rows + cols == LANES - 1)


def turn(matrix, array):
    return lax.dot_general(matrix, array, NT, preferred_element_type=jnp.float32)


def gate(left, right):
    return (left.astype(jnp.float32) * right.astype(jnp.float32)).astype(jnp.bfloat16)


def send_body(local, share, me_ref, key_ref, value_ref, grad_ref, query_ref, low_ref, high_ref, out_ref):
    seqs = out_ref.shape[0]
    per = LANES // local
    flip = reversal()
    row, lane = grid_of((share, LANES))
    for g in range(key_ref.shape[1] // LANES):
        at = slice(g * LANES, (g + 1) * LANES)
        product = gate(key_ref[:, at], value_ref[:, at]).T
        gated = jnp.dot(
            flip, gate(grad_ref[:, at], query_ref[:, at]), preferred_element_type=jnp.float32
        )
        gated = gated.astype(jnp.bfloat16).T
        low, high = low_ref[:, at], high_ref[:, at]
        taps = (
            jnp.where(lane < local, low, pltpu.roll(high, local, 1)),
            jnp.where(lane < local, pltpu.roll(low, local, 1), high),
        )
        for d in range(per):
            x, s = divmod(g * per + d, seqs)
            out_ref[s, x, :local, :] = product[d * local : (d + 1) * local]
            out_ref[s, x, local : 2 * local, :] = gated[d * local : (d + 1) * local]
            out_ref[s, x, 2 * local :, :] = taps[d].astype(jnp.bfloat16)


def send(key, value, grad, query, taps, local, share, seqs):
    length, channels = key.shape
    width = 4096
    message = 2 * local + share
    wide = width // local // seqs
    spec = pl.BlockSpec((length, width), lambda g, me: (0, g))
    return pl.pallas_call(
        functools.partial(send_body, local, share),
        grid_spec=pltpu.PrefetchScalarGridSpec(
            num_scalar_prefetch=1,
            grid=(channels // width,),
            in_specs=[spec] * 4
            + [
                pl.BlockSpec((share, width), lambda g, me: (me[0], g)),
                pl.BlockSpec((share, width), lambda g, me: (seqs + me[0], g)),
            ],
            out_specs=pl.BlockSpec((seqs, wide, message, LANES), lambda g, me: (0, g, 0, 0)),
        ),
        out_shape=jax.ShapeDtypeStruct(
            (seqs, channels // local // seqs, message, LANES), jnp.bfloat16
        ),
        compiler_params=params(60),
        cost_estimate=pl.CostEstimate(flops=0, bytes_accessed=14_000_000, transcendentals=0),
        name="send",
    )(lax.axis_index("dp").astype(jnp.int32).reshape(1), key, value, grad, query, taps, taps)


def rows_of(wide, block, c, seqs, blocks, group):
    return pl.ds(block * seqs * group + c, seqs, stride=group)


def both_body(seqs, blocks, prod_ref, grad_ref, taps_ref, out_ref, prod_wide, grad_wide, taps):
    group = prod_ref.shape[2]
    local = LANES // 2
    g = pl.program_id(0)

    @pl.when(g == 0)
    def _():
        row, lane = grid_of((local, LANES))
        for j in range(0, blocks, 2):
            lags = jnp.concatenate(
                [taps_ref[b, j + side] for side in (0, 1) for b in range(seqs)], axis=0
            )
            lags = lags.astype(jnp.float32).T
            low, high = lags[:local], lags[local:]
            taps[pl.ds(j, local, stride=blocks), :] = jnp.where(
                lane < local, low, pltpu.roll(high, local, 1)
            )
            taps[pl.ds(j + 1, local, stride=blocks), :] = jnp.where(
                lane < local, pltpu.roll(low, local, 1), high
            )

    for b in range(seqs):
        for j in range(blocks):
            at = slice((j * seqs + b) * group, (j * seqs + b + 1) * group)
            prod_wide[at, :] = prod_ref[b, j].astype(jnp.float32)
            grad_wide[at, :] = grad_ref[b, j].astype(jnp.float32)
    row, lane = grid_of((LANES, LANES))
    same_block = lane >= row
    pairs = blocks // 2

    def step(c, carry):
        def load(wide, block):
            return wide[rows_of(wide, block, c, seqs, blocks, group), :]

        tiles = []
        for i in range(pairs):
            o = pairs - 1 - i
            first = jnp.concatenate([load(prod_wide, 2 * i), load(prod_wide, 2 * i + 1)], axis=1)
            second = jnp.concatenate([load(grad_wide, 2 * o + 1), load(grad_wide, 2 * o)], axis=1)
            tiles.append(jnp.concatenate([first, second], axis=0).astype(jnp.bfloat16))
        lines = jnp.concatenate(tiles, axis=0)
        turned_before = jnp.zeros((LANES, LANES), jnp.float32)
        before = jnp.zeros((LANES, LANES), jnp.bfloat16)
        conv = [None] * pairs
        back = [None] * pairs

        def add(sums, i, piece):
            sums[i] = piece if sums[i] is None else sums[i] + piece

        for k in range(pairs):
            here = []
            for near in (2 * k, 2 * k + 1):
                line = taps[pl.ds((g * group + c) * blocks + near, 1), :]
                turned = pltpu.roll(
                    jnp.broadcast_to(line, (LANES, LANES)), 0, 1, stride=1, stride_axis=0
                )
                here.append(jnp.where(same_block, turned, turned_before).astype(jnp.bfloat16))
                turned_before = turned
            right = jnp.concatenate(
                [
                    jnp.concatenate(here, axis=1),
                    jnp.concatenate([before, here[0]], axis=1),
                ],
                axis=0,
            )
            before = here[1]
            part = jnp.dot(
                lines[: (pairs - k) * 2 * seqs], right, preferred_element_type=jnp.float32
            )
            for i in range(pairs - k):
                at = i * 2 * seqs
                add(conv, i + k, part[at : at + seqs])
                add(back, pairs - 1 - i - k, part[at + seqs : at + 2 * seqs])
        for i in range(pairs):
            for side in (0, 1):
                here = rows_of(prod_wide, 2 * i + side, c, seqs, blocks, group)
                prod_wide[here, :] = conv[i][:, side * LANES : (side + 1) * LANES]
                grad_wide[here, :] = back[i][:, (1 - side) * LANES : (2 - side) * LANES]
        return carry

    lax.fori_loop(0, group, step, 0, unroll=True)
    for b in range(seqs):
        for j in range(blocks):
            at = slice((j * seqs + b) * group, (j * seqs + b + 1) * group)
            out_ref[b, j, 0] = prod_wide[at, :].astype(jnp.bfloat16)
            out_ref[b, j, 1] = grad_wide[at, :].astype(jnp.bfloat16)


def both(received, local, share):
    seqs, blocks = received.shape[:2]
    group = 8
    steps = local // group
    size = seqs * blocks * group
    return pl.pallas_call(
        functools.partial(both_body, seqs, blocks),
        grid=(steps,),
        in_specs=[
            pl.BlockSpec((seqs, blocks, group, LANES), lambda g: (0, 0, g, 0)),
            pl.BlockSpec((seqs, blocks, group, LANES), lambda g: (0, 0, steps + g, 0)),
            pl.BlockSpec((seqs, blocks, share, LANES), lambda g: (0, 0, 2 * local // share, 0)),
        ],
        out_specs=pl.BlockSpec((seqs, blocks, 2, group, LANES), lambda g: (0, 0, 0, g, 0)),
        out_shape=jax.ShapeDtypeStruct((seqs, blocks, 2, local, LANES), jnp.bfloat16),
        scratch_shapes=[
            pltpu.VMEM((size, LANES), jnp.float32),
            pltpu.VMEM((size, LANES), jnp.float32),
            pltpu.VMEM((local * blocks, LANES), jnp.float32),
        ],
        compiler_params=params(60),
        cost_estimate=pl.CostEstimate(
            flops=20_000_000_000, bytes_accessed=10_000_000, transcendentals=0
        ),
        name="both",
    )(received, received, received)


def filter_body(seqs, blocks, prod_ref, grad_ref, out_ref, prod_wide, grad_wide, found):
    group = prod_ref.shape[2]
    same = identity()
    row, lane = grid_of((LANES, LANES))
    same_block = lane >= row
    for b in range(seqs):
        for j in range(blocks):
            at = slice((j * seqs + b) * group, (j * seqs + b + 1) * group)
            prod_wide[at, :] = prod_ref[b, j].astype(jnp.float32)
            grad_wide[at, :] = grad_ref[b, j].astype(jnp.float32)
    nothing = jnp.zeros((seqs, LANES), jnp.float32)

    def step(c, carry):
        def load(wide, block):
            return wide[rows_of(wide, block, c, seqs, blocks, group), :]

        prod = jnp.concatenate([load(prod_wide, j) for j in range(blocks)], axis=0)
        lines = turn(same, prod.astype(jnp.bfloat16)).astype(jnp.bfloat16)
        grad = [load(grad_wide, j) for j in range(blocks)] + [nothing] * 2
        twos = [
            jnp.concatenate([grad[j], grad[j + 1]], axis=0).astype(jnp.bfloat16)
            for j in range(blocks + 1)
        ]

        def shifted(k):
            return jnp.concatenate(
                [twos[min(j + k, blocks)] for j in range(0, blocks, 2)], axis=0
            )

        after = jnp.zeros((LANES, LANES), jnp.float32)
        for k in reversed(range(0, blocks, 2)):
            pair = jnp.concatenate([shifted(k), shifted(k + 1)], axis=1)
            part = jnp.dot(lines, pair, preferred_element_type=jnp.float32)
            for side in (1, 0):
                turned = pltpu.roll(
                    part[:, side * LANES : (side + 1) * LANES], 0, 1, stride=1, stride_axis=0
                )
                chosen = jnp.where(same_block, turned, after)
                found[pl.ds((k + side) * group + c, 1), :] = jnp.sum(chosen, axis=0, keepdims=True)
                after = turned
        return carry

    lax.fori_loop(0, group, step, 0, unroll=4)
    rows, cols = grid_of((LANES, LANES))
    flip = jnp.where(rows + cols == LANES - 1, 1.0, 0.0)
    lags = jnp.dot(
        found[...], flip, precision=lax.Precision.HIGHEST, preferred_element_type=jnp.float32
    )
    out_ref[...] = lags.reshape(blocks, group, LANES)


def filter_grad(received, local):
    seqs, blocks = received.shape[:2]
    group = 8
    steps = local // group
    size = seqs * blocks * group
    return pl.pallas_call(
        functools.partial(filter_body, seqs, blocks),
        grid=(steps,),
        in_specs=[
            pl.BlockSpec((seqs, blocks, group, LANES), lambda g: (0, 0, g, 0)),
            pl.BlockSpec((seqs, blocks, group, LANES), lambda g: (0, 0, steps + g, 0)),
        ],
        out_specs=pl.BlockSpec((blocks, group, LANES), lambda g: (0, g, 0)),
        out_shape=jax.ShapeDtypeStruct((blocks, local, LANES), jnp.float32),
        scratch_shapes=[pltpu.VMEM((size, LANES), jnp.float32)] * 2
        + [pltpu.VMEM((blocks * group, LANES), jnp.float32)],
        compiler_params=params(16),
        cost_estimate=pl.CostEstimate(
            flops=25_000_000_000, bytes_accessed=10_000_000, transcendentals=0
        ),
        name="filter_grad",
    )(received, received)


def finish_body(local, in_ref, grad_ref, value_ref, key_ref, query_out, key_out, value_out):
    flip = reversal()
    per = LANES // local
    seqs = in_ref.shape[0]
    for g in range(grad_ref.shape[1] // LANES):
        at = slice(g * LANES, (g + 1) * LANES)
        places = [divmod(g * per + d, seqs) for d in range(per)]
        conv = jnp.concatenate([in_ref[s, x, 0] for x, s in places], axis=0).T
        conv = conv.astype(jnp.float32)
        back = jnp.concatenate([in_ref[s, x, 1] for x, s in places], axis=0).T
        back = jnp.dot(flip, back, preferred_element_type=jnp.float32)
        query_out[:, at] = (conv * grad_ref[:, at].astype(jnp.float32)).astype(jnp.bfloat16)
        key_out[:, at] = (back * value_ref[:, at].astype(jnp.float32)).astype(jnp.bfloat16)
        value_out[:, at] = (back * key_ref[:, at].astype(jnp.float32)).astype(jnp.bfloat16)


def finish(received, grad, value, key):
    seqs, blocks, two, local, lanes = received.shape
    length, channels = key.shape
    width = 4096
    spec = pl.BlockSpec((length, width), lambda g: (0, g))
    shape = jax.ShapeDtypeStruct((length, channels), jnp.bfloat16)
    return pl.pallas_call(
        functools.partial(finish_body, local),
        grid=(channels // width,),
        in_specs=[
            pl.BlockSpec(
                (seqs, width // local // seqs, two, local, lanes), lambda g: (0, g, 0, 0, 0)
            )
        ]
        + [spec] * 3,
        out_specs=(spec,) * 3,
        out_shape=(shape,) * 3,
        compiler_params=params(60),
        cost_estimate=pl.CostEstimate(flops=0, bytes_accessed=20_000_000, transcendentals=0),
        name="finish",
    )(received, grad, value, key)


def exchange(array):
    seqs, blocks, *rest = array.shape
    flat = array.reshape(seqs * blocks, *rest)
    moved = lax.all_to_all(flat, ("dp", "ctx"), split_axis=0, concat_axis=0, tiled=True)
    return moved.reshape(array.shape)


def spread_lags(lags, seqs):
    me = lax.axis_index("dp")
    held = jnp.zeros_like(lags)
    for offset in range(seqs):
        piece = lax.dynamic_index_in_dim(lags, (me + offset) % seqs, 0, keepdims=True)
        if offset:
            piece = lax.ppermute(piece, "dp", [(s, (s + offset) % seqs) for s in range(seqs)])
        held = lax.dynamic_update_slice_in_dim(held, piece, (me - offset) % seqs, 0)
    return held


def on_device(seqs, blocks, query_act, key_act, value_act, grad_out, filter_taps):
    query, key, value, grad = query_act[0], key_act[0], value_act[0], grad_out[0]
    channels = key.shape[1]
    local = channels // (seqs * blocks)
    share = local // seqs
    received = exchange(send(key, value, grad, query, filter_taps, local, share, seqs))
    sums = both(received, local, share)
    returned = exchange(sums)
    received, sums = lax.optimization_barrier((received, sums))
    lags = filter_grad(received, local)
    lags = spread_lags(lags.reshape(seqs, blocks // seqs, local, LANES), seqs)
    grad_filter = lags.transpose(1, 3, 0, 2).reshape(blocks // seqs * LANES, seqs * local)
    grad_query, grad_key, grad_value = finish(returned, grad, value, key)
    return (grad_query[None], grad_key[None], grad_value[None], grad_filter)


def solution(mesh):
    seqs, blocks = mesh.shape["dp"], mesh.shape["ctx"]
    spec = P("dp", "ctx", None)
    return jax.shard_map(
        functools.partial(on_device, seqs, blocks),
        mesh=mesh,
        in_specs=(spec, spec, spec, spec, P("ctx", None)),
        out_specs=(spec, spec, spec, P("dp", "ctx")),
        check_vma=False,
    )
```

```python
import functools

import jax
import jax.numpy as jnp
from jax import lax
from jax.experimental import pallas as pl
from jax.experimental.pallas import tpu as pltpu
from jax.sharding import PartitionSpec as P

LANES = 128
GROUP = 16
PITCH = 24
NT = (((1,), (1,)), ((), ()))


def params(mib):
    return pltpu.CompilerParams(vmem_limit_bytes=mib * 1024 * 1024)


def grid_of(shape):
    return lax.broadcasted_iota(jnp.int32, shape, 0), lax.broadcasted_iota(jnp.int32, shape, 1)


def ones_where(condition):
    return jnp.where(condition, 1.0, 0.0).astype(jnp.bfloat16)


def identity():
    rows, cols = grid_of((LANES, LANES))
    return ones_where(rows == cols)


def reversal():
    rows, cols = grid_of((LANES, LANES))
    return ones_where(rows + cols == LANES - 1)


def turn(matrix, array):
    return lax.dot_general(matrix, array, NT, preferred_element_type=jnp.float32)


def gate(left, right):
    return (left.astype(jnp.float32) * right.astype(jnp.float32)).astype(jnp.bfloat16)


def send_body(local, share, me_ref, key_ref, value_ref, grad_ref, query_ref, low_ref, high_ref, out_ref):
    seqs = out_ref.shape[0]
    per = LANES // local
    flip = reversal()
    row, lane = grid_of((share, LANES))
    for g in range(key_ref.shape[1] // LANES):
        at = slice(g * LANES, (g + 1) * LANES)
        product = gate(key_ref[:, at], value_ref[:, at]).T
        gated = jnp.dot(
            flip, gate(grad_ref[:, at], query_ref[:, at]), preferred_element_type=jnp.float32
        )
        gated = gated.astype(jnp.bfloat16).T
        low, high = low_ref[:, at], high_ref[:, at]
        taps = (
            jnp.where(lane < local, low, pltpu.roll(high, local, 1)),
            jnp.where(lane < local, pltpu.roll(low, local, 1), high),
        )
        for d in range(per):
            x, s = divmod(g * per + d, seqs)
            out_ref[s, x, :local, :] = product[d * local : (d + 1) * local]
            out_ref[s, x, local : 2 * local, :] = gated[d * local : (d + 1) * local]
            out_ref[s, x, 2 * local :, :] = taps[d].astype(jnp.bfloat16)


def send(key, value, grad, query, taps, local, share, seqs):
    length, channels = key.shape
    width = 4096
    message = 2 * local + share
    wide = width // local // seqs
    spec = pl.BlockSpec((length, width), lambda g, me: (0, g))
    return pl.pallas_call(
        functools.partial(send_body, local, share),
        grid_spec=pltpu.PrefetchScalarGridSpec(
            num_scalar_prefetch=1,
            grid=(channels // width,),
            in_specs=[spec] * 4
            + [
                pl.BlockSpec((share, width), lambda g, me: (me[0], g)),
                pl.BlockSpec((share, width), lambda g, me: (seqs + me[0], g)),
            ],
            out_specs=pl.BlockSpec((seqs, wide, message, LANES), lambda g, me: (0, g, 0, 0)),
        ),
        out_shape=jax.ShapeDtypeStruct(
            (seqs, channels // local // seqs, message, LANES), jnp.bfloat16
        ),
        compiler_params=params(60),
        cost_estimate=pl.CostEstimate(flops=0, bytes_accessed=14_000_000, transcendentals=0),
        name="send",
    )(lax.axis_index("dp").astype(jnp.int32).reshape(1), key, value, grad, query, taps, taps)


def rows_of(block, c, seqs):
    return pl.ds(block * seqs * PITCH + c, seqs, stride=PITCH)


def both_body(seqs, blocks, prod_ref, grad_ref, taps_ref, out_ref, prod_wide, grad_wide, taps, made):
    group = prod_ref.shape[2]
    local = LANES // 2
    g = pl.program_id(0)

    @pl.when(g == 0)
    def _():
        row, lane = grid_of((local, LANES))
        for j in range(0, blocks, 2):
            lags = jnp.concatenate(
                [taps_ref[b, j + side] for side in (0, 1) for b in range(seqs)], axis=0
            )
            lags = lags.astype(jnp.float32).T
            low, high = lags[:local], lags[local:]
            taps[pl.ds(j, local, stride=blocks), :] = jnp.where(
                lane < local, low, pltpu.roll(high, local, 1)
            )
            taps[pl.ds(j + 1, local, stride=blocks), :] = jnp.where(
                lane < local, pltpu.roll(low, local, 1), high
            )

    for b in range(seqs):
        for j in range(blocks):
            start = (j * seqs + b) * PITCH
            at = slice(start, start + group)
            prod_wide[at, :] = prod_ref[b, j].astype(jnp.float32)
            grad_wide[at, :] = grad_ref[b, j].astype(jnp.float32)
    row, lane = grid_of((LANES, LANES))
    same_block = lane >= row
    pairs = blocks // 2

    def step(c, carry):
        def load(wide, block):
            return wide[rows_of(block, c, seqs), :]

        tiles = []
        for i in range(pairs):
            o = pairs - 1 - i
            first = jnp.concatenate([load(prod_wide, 2 * i), load(prod_wide, 2 * i + 1)], axis=1)
            second = jnp.concatenate([load(grad_wide, 2 * o + 1), load(grad_wide, 2 * o)], axis=1)
            tiles.append(jnp.concatenate([first, second], axis=0).astype(jnp.bfloat16))
        lines = jnp.concatenate(tiles, axis=0)
        turned_before = jnp.zeros((LANES, LANES), jnp.float32)
        before = jnp.zeros((LANES, LANES), jnp.bfloat16)
        made_slot = made.at[c % 2]
        for near in range(blocks):
            line = taps[pl.ds((g * group + c) * blocks + near, 1), :]
            turned = pltpu.roll(jnp.broadcast_to(line, (LANES, LANES)), 0, 1, stride=1, stride_axis=0)
            made_slot[near] = jnp.where(same_block, turned, turned_before).astype(jnp.bfloat16)
            turned_before = turned
        conv = [None] * pairs
        back = [None] * pairs

        def add(sums, i, piece):
            sums[i] = piece if sums[i] is None else sums[i] + piece

        for k in range(pairs):
            here = [made_slot[2 * k], made_slot[2 * k + 1]]
            right = jnp.concatenate(
                [
                    jnp.concatenate(here, axis=1),
                    jnp.concatenate([before, here[0]], axis=1),
                ],
                axis=0,
            )
            before = here[1]
            part = jnp.dot(
                lines[: (pairs - k) * 2 * seqs], right, preferred_element_type=jnp.float32
            )
            for i in range(pairs - k):
                at = i * 2 * seqs
                add(conv, i + k, part[at : at + seqs])
                add(back, pairs - 1 - i - k, part[at + seqs : at + 2 * seqs])
        for i in range(pairs):
            for side in (0, 1):
                here = rows_of(2 * i + side, c, seqs)
                prod_wide[here, :] = conv[i][:, side * LANES : (side + 1) * LANES]
                grad_wide[here, :] = back[i][:, (1 - side) * LANES : (2 - side) * LANES]
        return carry

    lax.fori_loop(0, group, step, 0, unroll=True)
    for b in range(seqs):
        for j in range(blocks):
            start = (j * seqs + b) * PITCH
            at = slice(start, start + group)
            out_ref[b, j, 0] = prod_wide[at, :].astype(jnp.bfloat16)
            out_ref[b, j, 1] = grad_wide[at, :].astype(jnp.bfloat16)


def both(received, local, share):
    seqs, blocks = received.shape[:2]
    group = GROUP
    steps = local // group
    size = (seqs * blocks + 1) * PITCH
    return pl.pallas_call(
        functools.partial(both_body, seqs, blocks),
        grid=(steps,),
        in_specs=[
            pl.BlockSpec((seqs, blocks, group, LANES), lambda g: (0, 0, g, 0)),
            pl.BlockSpec((seqs, blocks, group, LANES), lambda g: (0, 0, steps + g, 0)),
            pl.BlockSpec((seqs, blocks, share, LANES), lambda g: (0, 0, 2 * local // share, 0)),
        ],
        out_specs=pl.BlockSpec((seqs, blocks, 2, group, LANES), lambda g: (0, 0, 0, g, 0)),
        out_shape=jax.ShapeDtypeStruct((seqs, blocks, 2, local, LANES), jnp.bfloat16),
        scratch_shapes=[
            pltpu.VMEM((size, LANES), jnp.float32),
            pltpu.VMEM((size, LANES), jnp.float32),
            pltpu.VMEM(((local + 1) * blocks, LANES), jnp.float32),
            pltpu.VMEM((2, blocks, LANES, LANES), jnp.bfloat16),
        ],
        compiler_params=params(60),
        cost_estimate=pl.CostEstimate(
            flops=20_000_000_000, bytes_accessed=10_000_000, transcendentals=0
        ),
        name="both",
    )(received, received, received)


def filter_body(seqs, blocks, prod_ref, grad_ref, out_ref, prod_wide, grad_wide, found):
    group = prod_ref.shape[2]
    same = identity()
    row, lane = grid_of((LANES, LANES))
    same_block = lane >= row
    for b in range(seqs):
        for j in range(blocks):
            start = (j * seqs + b) * PITCH
            at = slice(start, start + group)
            prod_wide[at, :] = prod_ref[b, j].astype(jnp.float32)
            grad_wide[at, :] = grad_ref[b, j].astype(jnp.float32)
    nothing = jnp.zeros((seqs, LANES), jnp.float32)

    def step(c, carry):
        def load(wide, block):
            return wide[rows_of(block, c, seqs), :]

        prod = jnp.concatenate([load(prod_wide, j) for j in range(blocks)], axis=0)
        lines = turn(same, prod.astype(jnp.bfloat16)).astype(jnp.bfloat16)
        grad = [load(grad_wide, j) for j in range(blocks)] + [nothing] * 2
        twos = [
            jnp.concatenate([grad[j], grad[j + 1]], axis=0).astype(jnp.bfloat16)
            for j in range(blocks + 1)
        ]

        def shifted(k):
            return jnp.concatenate(
                [twos[min(j + k, blocks)] for j in range(0, blocks, 2)], axis=0
            )

        after = jnp.zeros((LANES, LANES), jnp.float32)
        for k in reversed(range(0, blocks, 2)):
            pair = jnp.concatenate([shifted(k), shifted(k + 1)], axis=1)
            part = jnp.dot(lines, pair, preferred_element_type=jnp.float32)
            for side in (1, 0):
                turned = pltpu.roll(
                    part[:, side * LANES : (side + 1) * LANES], 0, 1, stride=1, stride_axis=0
                )
                chosen = jnp.where(same_block, turned, after)
                found[pl.ds((k + side) * group + c, 1), :] = jnp.sum(chosen, axis=0, keepdims=True)
                after = turned
        return carry

    lax.fori_loop(0, group, step, 0, unroll=True)
    rows, cols = grid_of((LANES, LANES))
    flip = jnp.where(rows + cols == LANES - 1, 1.0, 0.0)
    lags = jnp.dot(
        found[...], flip, precision=lax.Precision.HIGHEST, preferred_element_type=jnp.float32
    )
    out_ref[...] = lags.astype(jnp.bfloat16).reshape(blocks, group, LANES)


def filter_grad(received, local):
    seqs, blocks = received.shape[:2]
    group = GROUP
    steps = local // group
    size = (seqs * blocks + 1) * PITCH
    return pl.pallas_call(
        functools.partial(filter_body, seqs, blocks),
        grid=(steps,),
        in_specs=[
            pl.BlockSpec((seqs, blocks, group, LANES), lambda g: (0, 0, g, 0)),
            pl.BlockSpec((seqs, blocks, group, LANES), lambda g: (0, 0, steps + g, 0)),
        ],
        out_specs=pl.BlockSpec((blocks, group, LANES), lambda g: (0, g, 0)),
        out_shape=jax.ShapeDtypeStruct((blocks, local, LANES), jnp.bfloat16),
        scratch_shapes=[pltpu.VMEM((size, LANES), jnp.float32)] * 2
        + [pltpu.VMEM((blocks * group, LANES), jnp.float32)],
        compiler_params=params(16),
        cost_estimate=pl.CostEstimate(
            flops=25_000_000_000, bytes_accessed=10_000_000, transcendentals=0
        ),
        name="filter_grad",
    )(received, received)


def finish_body(local, in_ref, grad_ref, value_ref, key_ref, query_out, key_out, value_out):
    flip = reversal()
    per = LANES // local
    seqs = in_ref.shape[0]
    for g in range(grad_ref.shape[1] // LANES):
        at = slice(g * LANES, (g + 1) * LANES)
        places = [divmod(g * per + d, seqs) for d in range(per)]
        conv = jnp.concatenate([in_ref[s, x, 0] for x, s in places], axis=0).T
        conv = conv.astype(jnp.float32)
        back = jnp.concatenate([in_ref[s, x, 1] for x, s in places], axis=0).T
        back = jnp.dot(flip, back, preferred_element_type=jnp.float32)
        query_out[:, at] = (conv * grad_ref[:, at].astype(jnp.float32)).astype(jnp.bfloat16)
        key_out[:, at] = (back * value_ref[:, at].astype(jnp.float32)).astype(jnp.bfloat16)
        value_out[:, at] = (back * key_ref[:, at].astype(jnp.float32)).astype(jnp.bfloat16)


def finish(received, grad, value, key):
    seqs, blocks, two, local, lanes = received.shape
    length, channels = key.shape
    width = 4096
    spec = pl.BlockSpec((length, width), lambda g: (0, g))
    shape = jax.ShapeDtypeStruct((length, channels), jnp.bfloat16)
    return pl.pallas_call(
        functools.partial(finish_body, local),
        grid=(channels // width,),
        in_specs=[
            pl.BlockSpec(
                (seqs, width // local // seqs, two, local, lanes), lambda g: (0, g, 0, 0, 0)
            )
        ]
        + [spec] * 3,
        out_specs=(spec,) * 3,
        out_shape=(shape,) * 3,
        compiler_params=params(60),
        cost_estimate=pl.CostEstimate(flops=0, bytes_accessed=20_000_000, transcendentals=0),
        name="finish",
    )(received, grad, value, key)


def exchange(array):
    seqs, blocks, *rest = array.shape
    flat = array.reshape(seqs * blocks, *rest)
    moved = lax.all_to_all(flat, ("dp", "ctx"), split_axis=0, concat_axis=0, tiled=True)
    return moved.reshape(array.shape)


def spread_lags(lags, seqs):
    me = lax.axis_index("dp")
    held = jnp.zeros_like(lags)
    for offset in range(seqs):
        piece = lax.dynamic_index_in_dim(lags, (me + offset) % seqs, 0, keepdims=True)
        if offset:
            piece = lax.ppermute(piece, "dp", [(s, (s + offset) % seqs) for s in range(seqs)])
        held = lax.dynamic_update_slice_in_dim(held, piece, (me - offset) % seqs, 0)
    return held


def on_device(seqs, blocks, query_act, key_act, value_act, grad_out, filter_taps):
    query, key, value, grad = query_act[0], key_act[0], value_act[0], grad_out[0]
    channels = key.shape[1]
    local = channels // (seqs * blocks)
    share = local // seqs
    received = exchange(send(key, value, grad, query, filter_taps, local, share, seqs))
    sums = both(received, local, share)
    returned = exchange(sums)
    received, sums = lax.optimization_barrier((received, sums))
    lags = filter_grad(received, local)
    lags = spread_lags(lags.reshape(seqs, blocks // seqs, local, LANES), seqs)
    grad_filter = lags.transpose(1, 3, 0, 2).reshape(blocks // seqs * LANES, seqs * local)
    grad_filter = grad_filter.astype(jnp.float32)
    grad_query, grad_key, grad_value = finish(returned, grad, value, key)
    return (grad_query[None], grad_key[None], grad_value[None], grad_filter)


def solution(mesh):
    seqs, blocks = mesh.shape["dp"], mesh.shape["ctx"]
    spec = P("dp", "ctx", None)
    return jax.shard_map(
        functools.partial(on_device, seqs, blocks),
        mesh=mesh,
        in_specs=(spec, spec, spec, spec, P("ctx", None)),
        out_specs=(spec, spec, spec, P("dp", "ctx")),
        check_vma=False,
    )
```

```python
import functools

import jax
import jax.numpy as jnp
from jax import lax
from jax.experimental import pallas as pl
from jax.experimental.pallas import tpu as pltpu
from jax.sharding import PartitionSpec as P

LANES = 128
GROUP = 16
PITCH = 24
NT = (((1,), (1,)), ((), ()))


def params(mib):
    return pltpu.CompilerParams(vmem_limit_bytes=mib * 1024 * 1024)


def grid_of(shape):
    return lax.broadcasted_iota(jnp.int32, shape, 0), lax.broadcasted_iota(jnp.int32, shape, 1)


def ones_where(condition):
    return jnp.where(condition, 1.0, 0.0).astype(jnp.bfloat16)


def identity():
    rows, cols = grid_of((LANES, LANES))
    return ones_where(rows == cols)


def reversal():
    rows, cols = grid_of((LANES, LANES))
    return ones_where(rows + cols == LANES - 1)


def turn(matrix, array):
    return lax.dot_general(matrix, array, NT, preferred_element_type=jnp.float32)


def gate(left, right):
    return (left.astype(jnp.float32) * right.astype(jnp.float32)).astype(jnp.bfloat16)


def send_body(local, share, me_ref, key_ref, value_ref, grad_ref, query_ref, low_ref, high_ref, out_ref):
    seqs = out_ref.shape[0]
    per = LANES // local
    flip = reversal()
    row, lane = grid_of((share, LANES))
    for g in range(key_ref.shape[1] // LANES):
        at = slice(g * LANES, (g + 1) * LANES)
        product = gate(key_ref[:, at], value_ref[:, at]).T
        gated = jnp.dot(
            flip, gate(grad_ref[:, at], query_ref[:, at]), preferred_element_type=jnp.float32
        )
        gated = gated.astype(jnp.bfloat16).T
        low, high = low_ref[:, at], high_ref[:, at]
        taps = (
            jnp.where(lane < local, low, pltpu.roll(high, local, 1)),
            jnp.where(lane < local, pltpu.roll(low, local, 1), high),
        )
        for d in range(per):
            x, s = divmod(g * per + d, seqs)
            out_ref[s, x, :local, :] = product[d * local : (d + 1) * local]
            out_ref[s, x, local : 2 * local, :] = gated[d * local : (d + 1) * local]
            out_ref[s, x, 2 * local :, :] = taps[d].astype(jnp.bfloat16)


def send(key, value, grad, query, taps, local, share, seqs):
    length, channels = key.shape
    width = 4096
    message = 2 * local + share
    wide = width // local // seqs
    spec = pl.BlockSpec((length, width), lambda g, me: (0, g))
    return pl.pallas_call(
        functools.partial(send_body, local, share),
        grid_spec=pltpu.PrefetchScalarGridSpec(
            num_scalar_prefetch=1,
            grid=(channels // width,),
            in_specs=[spec] * 4
            + [
                pl.BlockSpec((share, width), lambda g, me: (me[0], g)),
                pl.BlockSpec((share, width), lambda g, me: (seqs + me[0], g)),
            ],
            out_specs=pl.BlockSpec((seqs, wide, message, LANES), lambda g, me: (0, g, 0, 0)),
        ),
        out_shape=jax.ShapeDtypeStruct(
            (seqs, channels // local // seqs, message, LANES), jnp.bfloat16
        ),
        compiler_params=params(60),
        cost_estimate=pl.CostEstimate(flops=0, bytes_accessed=14_000_000, transcendentals=0),
        name="send",
    )(lax.axis_index("dp").astype(jnp.int32).reshape(1), key, value, grad, query, taps, taps)


def rows_of(block, c, seqs):
    return pl.ds(block * seqs * PITCH + c, seqs, stride=PITCH)


def both_body(seqs, blocks, prod_ref, grad_ref, taps_ref, out_ref, prod_wide, grad_wide, taps, made):
    group = prod_ref.shape[2]
    local = LANES // 2
    g = pl.program_id(0)

    @pl.when(g == 0)
    def _():
        row, lane = grid_of((local, LANES))
        for j in range(0, blocks, 2):
            lags = jnp.concatenate(
                [taps_ref[b, j + side] for side in (0, 1) for b in range(seqs)], axis=0
            )
            lags = lags.astype(jnp.float32).T
            low, high = lags[:local], lags[local:]
            taps[pl.ds(j, local, stride=blocks), :] = jnp.where(
                lane < local, low, pltpu.roll(high, local, 1)
            )
            taps[pl.ds(j + 1, local, stride=blocks), :] = jnp.where(
                lane < local, pltpu.roll(low, local, 1), high
            )

    for b in range(seqs):
        for j in range(blocks):
            start = (j * seqs + b) * PITCH
            at = slice(start, start + group)
            prod_wide[at, :] = prod_ref[b, j].astype(jnp.float32)
            grad_wide[at, :] = grad_ref[b, j].astype(jnp.float32)
    row, lane = grid_of((LANES, LANES))
    same_block = lane >= row
    pairs = blocks // 2

    def step(c, carry):
        def load(wide, block):
            return wide[rows_of(block, c, seqs), :]

        tiles = []
        for i in range(pairs):
            o = pairs - 1 - i
            first = jnp.concatenate([load(prod_wide, 2 * i), load(prod_wide, 2 * i + 1)], axis=1)
            second = jnp.concatenate([load(grad_wide, 2 * o + 1), load(grad_wide, 2 * o)], axis=1)
            tiles.append(jnp.concatenate([first, second], axis=0).astype(jnp.bfloat16))
        lines = jnp.concatenate(tiles, axis=0)
        turned_before = jnp.zeros((LANES, LANES), jnp.float32)
        before = jnp.zeros((LANES, LANES), jnp.bfloat16)
        made_slot = made.at[c % 2]
        for near in range(blocks):
            line = taps[pl.ds((g * group + c) * blocks + near, 1), :]
            turned = pltpu.roll(jnp.broadcast_to(line, (LANES, LANES)), 0, 1, stride=1, stride_axis=0)
            made_slot[near] = jnp.where(same_block, turned, turned_before).astype(jnp.bfloat16)
            turned_before = turned
        conv = [None] * pairs
        back = [None] * pairs

        def add(sums, i, piece):
            sums[i] = piece if sums[i] is None else sums[i] + piece

        for k in range(pairs):
            here = [made_slot[2 * k], made_slot[2 * k + 1]]
            right = jnp.concatenate(
                [
                    jnp.concatenate(here, axis=1),
                    jnp.concatenate([before, here[0]], axis=1),
                ],
                axis=0,
            )
            before = here[1]
            part = jnp.dot(
                lines[: (pairs - k) * 2 * seqs], right, preferred_element_type=jnp.float32
            )
            for i in range(pairs - k):
                at = i * 2 * seqs
                add(conv, i + k, part[at : at + seqs])
                add(back, pairs - 1 - i - k, part[at + seqs : at + 2 * seqs])
        for i in range(pairs):
            for side in (0, 1):
                here = rows_of(2 * i + side, c, seqs)
                prod_wide[here, :] = conv[i][:, side * LANES : (side + 1) * LANES]
                grad_wide[here, :] = back[i][:, (1 - side) * LANES : (2 - side) * LANES]
        return carry

    lax.fori_loop(0, group, step, 0, unroll=True)
    for b in range(seqs):
        for j in range(blocks):
            start = (j * seqs + b) * PITCH
            at = slice(start, start + group)
            out_ref[b, j, 0] = prod_wide[at, :].astype(jnp.bfloat16)
            out_ref[b, j, 1] = grad_wide[at, :].astype(jnp.bfloat16)


def both(received, local, share):
    seqs, blocks = received.shape[:2]
    group = GROUP
    steps = local // group
    size = (seqs * blocks + 1) * PITCH
    return pl.pallas_call(
        functools.partial(both_body, seqs, blocks),
        grid=(steps,),
        in_specs=[
            pl.BlockSpec((seqs, blocks, group, LANES), lambda g: (0, 0, g, 0)),
            pl.BlockSpec((seqs, blocks, group, LANES), lambda g: (0, 0, steps + g, 0)),
            pl.BlockSpec((seqs, blocks, share, LANES), lambda g: (0, 0, 2 * local // share, 0)),
        ],
        out_specs=pl.BlockSpec((seqs, blocks, 2, group, LANES), lambda g: (0, 0, 0, g, 0)),
        out_shape=jax.ShapeDtypeStruct((seqs, blocks, 2, local, LANES), jnp.bfloat16),
        scratch_shapes=[
            pltpu.VMEM((size, LANES), jnp.float32),
            pltpu.VMEM((size, LANES), jnp.float32),
            pltpu.VMEM(((local + 1) * blocks, LANES), jnp.float32),
            pltpu.VMEM((2, blocks, LANES, LANES), jnp.bfloat16),
        ],
        compiler_params=params(60),
        cost_estimate=pl.CostEstimate(
            flops=20_000_000_000, bytes_accessed=10_000_000, transcendentals=0
        ),
        name="both",
    )(received, received, received)


def filter_body(seqs, blocks, prod_ref, grad_ref, out_ref, prod_wide, grad_wide, found):
    group = prod_ref.shape[2]
    same = identity()
    row, lane = grid_of((LANES, LANES))
    same_block = lane >= row
    for b in range(seqs):
        for j in range(blocks):
            start = (j * seqs + b) * PITCH
            at = slice(start, start + group)
            prod_wide[at, :] = prod_ref[b, j].astype(jnp.float32)
            grad_wide[at, :] = grad_ref[b, j].astype(jnp.float32)
    nothing = jnp.zeros((seqs, LANES), jnp.float32)

    def step(c, carry):
        def load(wide, block):
            return wide[rows_of(block, c, seqs), :]

        prod = jnp.concatenate([load(prod_wide, j) for j in range(blocks)], axis=0)
        lines = turn(same, prod.astype(jnp.bfloat16)).astype(jnp.bfloat16)
        grad = [load(grad_wide, j) for j in range(blocks)] + [nothing] * 2
        twos = [
            jnp.concatenate([grad[j], grad[j + 1]], axis=0).astype(jnp.bfloat16)
            for j in range(blocks + 1)
        ]

        def shifted(k):
            return jnp.concatenate(
                [twos[min(j + k, blocks)] for j in range(0, blocks, 2)], axis=0
            )

        after = jnp.zeros((LANES, LANES), jnp.float32)
        for k in reversed(range(0, blocks, 2)):
            pair = jnp.concatenate([shifted(k), shifted(k + 1)], axis=1)
            part = jnp.dot(lines, pair, preferred_element_type=jnp.float32)
            for side in (1, 0):
                turned = pltpu.roll(
                    part[:, side * LANES : (side + 1) * LANES], 0, 1, stride=1, stride_axis=0
                )
                chosen = jnp.where(same_block, turned, after)
                found[pl.ds((k + side) * group + c, 1), :] = jnp.sum(chosen, axis=0, keepdims=True)
                after = turned
        return carry

    lax.fori_loop(0, group, step, 0, unroll=True)
    rows, cols = grid_of((LANES, LANES))
    flip = jnp.where(rows + cols == LANES - 1, 1.0, 0.0)
    lags = jnp.dot(
        found[...], flip, precision=lax.Precision.HIGHEST, preferred_element_type=jnp.float32
    )
    out_ref[...] = lags.astype(jnp.bfloat16).reshape(blocks, group, LANES)


def filter_grad(received, local):
    seqs, blocks = received.shape[:2]
    group = GROUP
    steps = local // group
    size = (seqs * blocks + 1) * PITCH
    return pl.pallas_call(
        functools.partial(filter_body, seqs, blocks),
        grid=(steps,),
        in_specs=[
            pl.BlockSpec((seqs, blocks, group, LANES), lambda g: (0, 0, g, 0)),
            pl.BlockSpec((seqs, blocks, group, LANES), lambda g: (0, 0, steps + g, 0)),
        ],
        out_specs=pl.BlockSpec((blocks, group, LANES), lambda g: (0, g, 0)),
        out_shape=jax.ShapeDtypeStruct((blocks, local, LANES), jnp.bfloat16),
        scratch_shapes=[pltpu.VMEM((size, LANES), jnp.float32)] * 2
        + [pltpu.VMEM((blocks * group, LANES), jnp.float32)],
        compiler_params=params(16),
        cost_estimate=pl.CostEstimate(
            flops=25_000_000_000, bytes_accessed=10_000_000, transcendentals=0
        ),
        name="filter_grad",
    )(received, received)


def finish_body(local, in_ref, grad_ref, value_ref, key_ref, query_out, key_out, value_out):
    flip = reversal()
    per = LANES // local
    seqs = in_ref.shape[0]
    for g in range(grad_ref.shape[1] // LANES):
        at = slice(g * LANES, (g + 1) * LANES)
        places = [divmod(g * per + d, seqs) for d in range(per)]
        conv = jnp.concatenate([in_ref[s, x, 0] for x, s in places], axis=0).T
        conv = conv.astype(jnp.float32)
        back = jnp.concatenate([in_ref[s, x, 1] for x, s in places], axis=0).T
        back = jnp.dot(flip, back, preferred_element_type=jnp.float32)
        query_out[:, at] = (conv * grad_ref[:, at].astype(jnp.float32)).astype(jnp.bfloat16)
        key_out[:, at] = (back * value_ref[:, at].astype(jnp.float32)).astype(jnp.bfloat16)
        value_out[:, at] = (back * key_ref[:, at].astype(jnp.float32)).astype(jnp.bfloat16)


def finish(received, grad, value, key):
    seqs, blocks, two, local, lanes = received.shape
    length, channels = key.shape
    width = 4096
    spec = pl.BlockSpec((length, width), lambda g: (0, g))
    shape = jax.ShapeDtypeStruct((length, channels), jnp.bfloat16)
    return pl.pallas_call(
        functools.partial(finish_body, local),
        grid=(channels // width,),
        in_specs=[
            pl.BlockSpec(
                (seqs, width // local // seqs, two, local, lanes), lambda g: (0, g, 0, 0, 0)
            )
        ]
        + [spec] * 3,
        out_specs=(spec,) * 3,
        out_shape=(shape,) * 3,
        compiler_params=params(60),
        cost_estimate=pl.CostEstimate(flops=0, bytes_accessed=20_000_000, transcendentals=0),
        name="finish",
    )(received, grad, value, key)


def exchange(array):
    seqs, blocks, *rest = array.shape
    flat = array.reshape(seqs * blocks, *rest)
    moved = lax.all_to_all(flat, ("dp", "ctx"), split_axis=0, concat_axis=0, tiled=True)
    return moved.reshape(array.shape)


def spread_lags(lags, seqs):
    pair, side = lax.axis_index("dp") // 2, lax.axis_index("dp") % 2
    pairs = seqs // 2
    lags = lags.reshape(pairs, 2, *lags.shape[1:])
    mine = lax.dynamic_slice_in_dim(lags, side, 1, 1)
    theirs = lax.dynamic_slice_in_dim(lags, 1 - side, 1, 1)
    theirs = lax.ppermute(theirs, "dp", [(d, d + 1 - 2 * (d % 2)) for d in range(seqs)])
    first = side == 0
    joined = jnp.concatenate(
        [jnp.where(first, mine, theirs), jnp.where(first, theirs, mine)], axis=1
    )
    held = jnp.zeros_like(joined)
    for offset in range(pairs):
        piece = lax.dynamic_slice_in_dim(joined, (pair + offset) % pairs, 1, 0)
        if offset:
            piece = lax.ppermute(piece, "dp", [(d, (d + 2 * offset) % seqs) for d in range(seqs)])
        held = lax.dynamic_update_slice_in_dim(held, piece, (pair - offset) % pairs, 0)
    return held.reshape(seqs, *held.shape[2:])


def on_device(seqs, blocks, query_act, key_act, value_act, grad_out, filter_taps):
    query, key, value, grad = query_act[0], key_act[0], value_act[0], grad_out[0]
    channels = key.shape[1]
    local = channels // (seqs * blocks)
    share = local // seqs
    received = exchange(send(key, value, grad, query, filter_taps, local, share, seqs))
    sums = both(received, local, share)
    returned = exchange(sums)
    received, sums = lax.optimization_barrier((received, sums))
    lags = filter_grad(received, local)
    lags = spread_lags(lags.reshape(seqs, blocks // seqs, local, LANES), seqs)
    grad_filter = lags.transpose(1, 3, 0, 2).reshape(blocks // seqs * LANES, seqs * local)
    grad_filter = grad_filter.astype(jnp.float32)
    grad_query, grad_key, grad_value = finish(returned, grad, value, key)
    return (grad_query[None], grad_key[None], grad_value[None], grad_filter)


def solution(mesh):
    seqs, blocks = mesh.shape["dp"], mesh.shape["ctx"]
    spec = P("dp", "ctx", None)
    return jax.shard_map(
        functools.partial(on_device, seqs, blocks),
        mesh=mesh,
        in_specs=(spec, spec, spec, spec, P("ctx", None)),
        out_specs=(spec, spec, spec, P("dp", "ctx")),
        check_vma=False,
    )
```

```python
import functools

import jax
import jax.numpy as jnp
from jax import lax
from jax.experimental import pallas as pl
from jax.experimental.pallas import tpu as pltpu
from jax.sharding import PartitionSpec as P

LANES = 128
GROUP = 16
PITCH = 24
NT = (((1,), (1,)), ((), ()))


def params(mib):
    return pltpu.CompilerParams(vmem_limit_bytes=mib * 1024 * 1024)


def grid_of(shape):
    return lax.broadcasted_iota(jnp.int32, shape, 0), lax.broadcasted_iota(jnp.int32, shape, 1)


def ones_where(condition):
    return jnp.where(condition, 1.0, 0.0).astype(jnp.bfloat16)


def identity():
    rows, cols = grid_of((LANES, LANES))
    return ones_where(rows == cols)


def reversal():
    rows, cols = grid_of((LANES, LANES))
    return ones_where(rows + cols == LANES - 1)


def turn(matrix, array):
    return lax.dot_general(matrix, array, NT, preferred_element_type=jnp.float32)


def gate(left, right):
    return (left.astype(jnp.float32) * right.astype(jnp.float32)).astype(jnp.bfloat16)


def send_body(local, share, me_ref, key_ref, value_ref, grad_ref, query_ref, low_ref, high_ref, out_ref):
    seqs = out_ref.shape[0]
    per = LANES // local
    flip = reversal()
    row, lane = grid_of((share, LANES))
    for g in range(key_ref.shape[1] // LANES):
        at = slice(g * LANES, (g + 1) * LANES)
        product = gate(key_ref[:, at], value_ref[:, at]).T
        gated = jnp.dot(
            flip, gate(grad_ref[:, at], query_ref[:, at]), preferred_element_type=jnp.float32
        )
        gated = gated.astype(jnp.bfloat16).T
        low, high = low_ref[:, at], high_ref[:, at]
        taps = (
            jnp.where(lane < local, low, pltpu.roll(high, local, 1)),
            jnp.where(lane < local, pltpu.roll(low, local, 1), high),
        )
        for d in range(per):
            x, s = divmod(g * per + d, seqs)
            out_ref[s, x, :local, :] = product[d * local : (d + 1) * local]
            out_ref[s, x, local : 2 * local, :] = gated[d * local : (d + 1) * local]
            out_ref[s, x, 2 * local :, :] = taps[d].astype(jnp.bfloat16)


def send(key, value, grad, query, taps, local, share, seqs):
    length, channels = key.shape
    width = 4096
    message = 2 * local + share
    wide = width // local // seqs
    spec = pl.BlockSpec((length, width), lambda g, me: (0, g))
    return pl.pallas_call(
        functools.partial(send_body, local, share),
        grid_spec=pltpu.PrefetchScalarGridSpec(
            num_scalar_prefetch=1,
            grid=(channels // width,),
            in_specs=[spec] * 4
            + [
                pl.BlockSpec((share, width), lambda g, me: (me[0], g)),
                pl.BlockSpec((share, width), lambda g, me: (seqs + me[0], g)),
            ],
            out_specs=pl.BlockSpec((seqs, wide, message, LANES), lambda g, me: (0, g, 0, 0)),
        ),
        out_shape=jax.ShapeDtypeStruct(
            (seqs, channels // local // seqs, message, LANES), jnp.bfloat16
        ),
        compiler_params=params(60),
        cost_estimate=pl.CostEstimate(flops=0, bytes_accessed=14_000_000, transcendentals=0),
        name="send",
    )(lax.axis_index("dp").astype(jnp.int32).reshape(1), key, value, grad, query, taps, taps)


def rows_of(block, c, seqs):
    return pl.ds(block * seqs * PITCH + c, seqs, stride=PITCH)


def both_body(seqs, blocks, prod_ref, grad_ref, taps_ref, out_ref, prod_wide, grad_wide, taps, made):
    group = prod_ref.shape[2]
    local = LANES // 2
    g = pl.program_id(0)

    @pl.when(g == 0)
    def _():
        row, lane = grid_of((local, LANES))
        for j in range(0, blocks, 2):
            lags = jnp.concatenate(
                [taps_ref[b, j + side] for side in (0, 1) for b in range(seqs)], axis=0
            )
            lags = lags.astype(jnp.float32).T
            low, high = lags[:local], lags[local:]
            taps[pl.ds(j, local, stride=blocks), :] = jnp.where(
                lane < local, low, pltpu.roll(high, local, 1)
            )
            taps[pl.ds(j + 1, local, stride=blocks), :] = jnp.where(
                lane < local, pltpu.roll(low, local, 1), high
            )

    for b in range(seqs):
        for j in range(blocks):
            start = (j * seqs + b) * PITCH
            at = slice(start, start + group)
            prod_wide[at, :] = prod_ref[b, j].astype(jnp.float32)
            grad_wide[at, :] = grad_ref[b, j].astype(jnp.float32)
    row, lane = grid_of((LANES, LANES))
    same_block = lane >= row
    pairs = blocks // 2

    def step(c, carry):
        def load(wide, block):
            return wide[rows_of(block, c, seqs), :]

        tiles = []
        for i in range(pairs):
            o = pairs - 1 - i
            first = jnp.concatenate([load(prod_wide, 2 * i), load(prod_wide, 2 * i + 1)], axis=1)
            second = jnp.concatenate([load(grad_wide, 2 * o + 1), load(grad_wide, 2 * o)], axis=1)
            tiles.append(jnp.concatenate([first, second], axis=0).astype(jnp.bfloat16))
        lines = jnp.concatenate(tiles, axis=0)
        turned_before = jnp.zeros((LANES, LANES), jnp.float32)
        before = jnp.zeros((LANES, LANES), jnp.bfloat16)
        made_slot = made.at[c % 2]
        for near in range(blocks):
            line = taps[pl.ds((g * group + c) * blocks + near, 1), :]
            turned = pltpu.roll(jnp.broadcast_to(line, (LANES, LANES)), 0, 1, stride=1, stride_axis=0)
            made_slot[near] = jnp.where(same_block, turned, turned_before).astype(jnp.bfloat16)
            turned_before = turned
        conv = [None] * pairs
        back = [None] * pairs

        def add(sums, i, piece):
            sums[i] = piece if sums[i] is None else sums[i] + piece

        for k in range(pairs):
            here = [made_slot[2 * k], made_slot[2 * k + 1]]
            right = jnp.concatenate(
                [
                    jnp.concatenate(here, axis=1),
                    jnp.concatenate([before, here[0]], axis=1),
                ],
                axis=0,
            )
            before = here[1]
            part = jnp.dot(
                lines[: (pairs - k) * 2 * seqs], right, preferred_element_type=jnp.float32
            )
            for i in range(pairs - k):
                at = i * 2 * seqs
                add(conv, i + k, part[at : at + seqs])
                add(back, pairs - 1 - i - k, part[at + seqs : at + 2 * seqs])
        for i in range(pairs):
            for side in (0, 1):
                here = rows_of(2 * i + side, c, seqs)
                prod_wide[here, :] = conv[i][:, side * LANES : (side + 1) * LANES]
                grad_wide[here, :] = back[i][:, (1 - side) * LANES : (2 - side) * LANES]
        return carry

    lax.fori_loop(0, group, step, 0, unroll=True)
    for b in range(seqs):
        for j in range(blocks):
            start = (j * seqs + b) * PITCH
            at = slice(start, start + group)
            out_ref[b, j, 0] = prod_wide[at, :].astype(jnp.bfloat16)
            out_ref[b, j, 1] = grad_wide[at, :].astype(jnp.bfloat16)


def both(received, local, share):
    seqs, blocks = received.shape[:2]
    group = GROUP
    steps = local // group
    size = (seqs * blocks + 1) * PITCH
    return pl.pallas_call(
        functools.partial(both_body, seqs, blocks),
        grid=(steps,),
        in_specs=[
            pl.BlockSpec((seqs, blocks, group, LANES), lambda g: (0, 0, g, 0)),
            pl.BlockSpec((seqs, blocks, group, LANES), lambda g: (0, 0, steps + g, 0)),
            pl.BlockSpec((seqs, blocks, share, LANES), lambda g: (0, 0, 2 * local // share, 0)),
        ],
        out_specs=pl.BlockSpec((seqs, blocks, 2, group, LANES), lambda g: (0, 0, 0, g, 0)),
        out_shape=jax.ShapeDtypeStruct((seqs, blocks, 2, local, LANES), jnp.bfloat16),
        scratch_shapes=[
            pltpu.VMEM((size, LANES), jnp.float32),
            pltpu.VMEM((size, LANES), jnp.float32),
            pltpu.VMEM(((local + 1) * blocks, LANES), jnp.float32),
            pltpu.VMEM((2, blocks, LANES, LANES), jnp.bfloat16),
        ],
        compiler_params=params(60),
        cost_estimate=pl.CostEstimate(
            flops=20_000_000_000, bytes_accessed=10_000_000, transcendentals=0
        ),
        name="both",
    )(received, received, received)


def filter_body(seqs, blocks, prod_ref, grad_ref, out_ref, prod_wide, grad_wide, found):
    group = prod_ref.shape[2]
    same = identity()
    row, lane = grid_of((LANES, LANES))
    same_block = lane >= row
    for b in range(seqs):
        for j in range(blocks):
            start = (j * seqs + b) * PITCH
            at = slice(start, start + group)
            prod_wide[at, :] = prod_ref[b, j].astype(jnp.float32)
            grad_wide[at, :] = grad_ref[b, j].astype(jnp.float32)
    nothing = jnp.zeros((seqs, LANES), jnp.float32)

    def step(c, carry):
        def load(wide, block):
            return wide[rows_of(block, c, seqs), :]

        prod = jnp.concatenate([load(prod_wide, j) for j in range(blocks)], axis=0)
        lines = turn(same, prod.astype(jnp.bfloat16)).astype(jnp.bfloat16)
        grad = [load(grad_wide, j) for j in range(blocks)] + [nothing] * 2
        twos = [
            jnp.concatenate([grad[j], grad[j + 1]], axis=0).astype(jnp.bfloat16)
            for j in range(blocks + 1)
        ]

        def shifted(k):
            return jnp.concatenate(
                [twos[min(j + k, blocks)] for j in range(0, blocks, 2)], axis=0
            )

        after = jnp.zeros((LANES, LANES), jnp.float32)
        for k in reversed(range(0, blocks, 2)):
            pair = jnp.concatenate([shifted(k), shifted(k + 1)], axis=1)
            part = jnp.dot(lines, pair, preferred_element_type=jnp.float32)
            for side in (1, 0):
                turned = pltpu.roll(
                    part[:, side * LANES : (side + 1) * LANES], 0, 1, stride=1, stride_axis=0
                )
                chosen = jnp.where(same_block, turned, after)
                found[pl.ds((k + side) * group + c, 1), :] = jnp.sum(chosen, axis=0, keepdims=True)
                after = turned
        return carry

    lax.fori_loop(0, group, step, 0, unroll=True)
    rows, cols = grid_of((LANES, LANES))
    flip = jnp.where(rows + cols == LANES - 1, 1.0, 0.0)
    lags = jnp.dot(
        found[...], flip, precision=lax.Precision.HIGHEST, preferred_element_type=jnp.float32
    )
    out_ref[...] = lags.astype(jnp.bfloat16).reshape(blocks, group, LANES)


def filter_grad(received, local):
    seqs, blocks = received.shape[:2]
    group = GROUP
    steps = local // group
    size = (seqs * blocks + 1) * PITCH
    return pl.pallas_call(
        functools.partial(filter_body, seqs, blocks),
        grid=(steps,),
        in_specs=[
            pl.BlockSpec((seqs, blocks, group, LANES), lambda g: (0, 0, g, 0)),
            pl.BlockSpec((seqs, blocks, group, LANES), lambda g: (0, 0, steps + g, 0)),
        ],
        out_specs=pl.BlockSpec((blocks, group, LANES), lambda g: (0, g, 0)),
        out_shape=jax.ShapeDtypeStruct((blocks, local, LANES), jnp.bfloat16),
        scratch_shapes=[pltpu.VMEM((size, LANES), jnp.float32)] * 2
        + [pltpu.VMEM((blocks * group, LANES), jnp.float32)],
        compiler_params=params(16),
        cost_estimate=pl.CostEstimate(
            flops=25_000_000_000, bytes_accessed=10_000_000, transcendentals=0
        ),
        name="filter_grad",
    )(received, received)


def finish_body(local, in_ref, grad_ref, value_ref, key_ref, query_out, key_out, value_out):
    flip = reversal()
    per = LANES // local
    seqs = in_ref.shape[0]
    for g in range(grad_ref.shape[1] // LANES):
        at = slice(g * LANES, (g + 1) * LANES)
        places = [divmod(g * per + d, seqs) for d in range(per)]
        conv = jnp.concatenate([in_ref[s, x, 0] for x, s in places], axis=0).T
        conv = conv.astype(jnp.float32)
        back = jnp.concatenate([in_ref[s, x, 1] for x, s in places], axis=0).T
        back = jnp.dot(flip, back, preferred_element_type=jnp.float32)
        query_out[:, at] = (conv * grad_ref[:, at].astype(jnp.float32)).astype(jnp.bfloat16)
        key_out[:, at] = (back * value_ref[:, at].astype(jnp.float32)).astype(jnp.bfloat16)
        value_out[:, at] = (back * key_ref[:, at].astype(jnp.float32)).astype(jnp.bfloat16)


def finish(received, grad, value, key):
    seqs, blocks, two, local, lanes = received.shape
    length, channels = key.shape
    width = 4096
    spec = pl.BlockSpec((length, width), lambda g: (0, g))
    shape = jax.ShapeDtypeStruct((length, channels), jnp.bfloat16)
    return pl.pallas_call(
        functools.partial(finish_body, local),
        grid=(channels // width,),
        in_specs=[
            pl.BlockSpec(
                (seqs, width // local // seqs, two, local, lanes), lambda g: (0, g, 0, 0, 0)
            )
        ]
        + [spec] * 3,
        out_specs=(spec,) * 3,
        out_shape=(shape,) * 3,
        compiler_params=params(60),
        cost_estimate=pl.CostEstimate(flops=0, bytes_accessed=20_000_000, transcendentals=0),
        name="finish",
    )(received, grad, value, key)


def exchange(array):
    seqs, blocks, *rest = array.shape
    flat = array.reshape(seqs * blocks, *rest)
    moved = lax.all_to_all(flat, ("dp", "ctx"), split_axis=0, concat_axis=0, tiled=True)
    return moved.reshape(array.shape)


def spread_lags(lags, seqs):
    pair, side = lax.axis_index("dp") // 2, lax.axis_index("dp") % 2
    pairs = seqs // 2
    lags = lags.reshape(pairs, 2, *lags.shape[1:])
    mine = lax.dynamic_slice_in_dim(lags, side, 1, 1)
    theirs = lax.dynamic_slice_in_dim(lags, 1 - side, 1, 1)
    theirs = lax.ppermute(theirs, "dp", [(d, d + 1 - 2 * (d % 2)) for d in range(seqs)])
    first = side == 0
    joined = jnp.concatenate(
        [jnp.where(first, mine, theirs), jnp.where(first, theirs, mine)], axis=1
    )
    came = []
    for offset in range(pairs):
        piece = lax.dynamic_slice_in_dim(joined, (pair + offset) % pairs, 1, 0)
        if offset:
            piece = lax.ppermute(piece, "dp", [(d, (d + 2 * offset) % seqs) for d in range(seqs)])
        came.append(piece)
    return came


def gather_lags(came):
    pair, pairs = lax.axis_index("dp") // 2, len(came)
    held = jnp.zeros((pairs, *came[0].shape[1:]), came[0].dtype)
    for offset, piece in enumerate(came):
        held = lax.dynamic_update_slice_in_dim(held, piece, (pair - offset) % pairs, 0)
    return held.reshape(2 * pairs, *held.shape[2:])


def on_device(seqs, blocks, query_act, key_act, value_act, grad_out, filter_taps):
    query, key, value, grad = query_act[0], key_act[0], value_act[0], grad_out[0]
    channels = key.shape[1]
    local = channels // (seqs * blocks)
    share = local // seqs
    received = exchange(send(key, value, grad, query, filter_taps, local, share, seqs))
    sums = both(received, local, share)
    returned = exchange(sums)
    received, sums = lax.optimization_barrier((received, sums))
    lags = filter_grad(received, local)
    came = spread_lags(lags.reshape(seqs, blocks // seqs, local, LANES), seqs)
    grad_query, grad_key, grad_value = finish(returned, grad, value, key)
    came, grad_query = lax.optimization_barrier((came, grad_query))
    lags = gather_lags(came)
    grad_filter = lags.transpose(1, 3, 0, 2).reshape(blocks // seqs * LANES, seqs * local)
    grad_filter = grad_filter.astype(jnp.float32)
    return (grad_query[None], grad_key[None], grad_value[None], grad_filter)


def solution(mesh):
    seqs, blocks = mesh.shape["dp"], mesh.shape["ctx"]
    spec = P("dp", "ctx", None)
    return jax.shard_map(
        functools.partial(on_device, seqs, blocks),
        mesh=mesh,
        in_specs=(spec, spec, spec, spec, P("ctx", None)),
        out_specs=(spec, spec, spec, P("dp", "ctx")),
        check_vma=False,
    )
```
